256 devices in a mesh: section: 8 (over y, z_lo), replica: 32 (over x, z_hi, core).
Axes of the slice: x: 4, y: 4, z: 8 (z_hi: 4, z_lo: 2; z = z_hi * 2 + z_lo), core: 2. Of those that a mesh axis runs over, the one named last changes fastest.
Arguments:
- stream: bfloat16 [32, 192, 5120], P('replica'), may hold values from -6 to 6
- doc_ids: int32 [32, 192], P('replica'), may hold values from 0 to 23, never falling along the last dimension, each value on 1 to 96 neighbouring positions
- gain: bfloat16 [32, 8, 5120], P('replica', 'section'), may hold values from 0.099609375 to 1.8984375
- down: bfloat16 [32, 8, 5120, 256], P('replica', 'section'), may hold values from -0.078125 to 0.078125
- up: bfloat16 [32, 8, 5120, 256], P('replica', 'section'), may hold values from -0.375 to 0.375
- round_exponent: int32 [1], replicated, may hold values from 0 to 1023
Outputs:
- gradients: bfloat16 [32, 8, 2, 5120, 256], P('replica', 'section')
The draws below stay inside these ranges and needn't reach their ends.
All inputs are finite; a program needn't handle non-finite values.
Results may differ from the reference program's by a relative error of at most 0.017.
Values may be sent and summed in bfloat16 or wider, within the bound.
No kernel may reach another device: no remote copies, remote signals or barrier semaphores. Data moves between devices by JAX's collectives and lax.ppermute only.
A program may use at most 128 MiB of HBM per device.

```python
import math
import jax
import jax.numpy as jnp
import numpy as np
from jax import lax

D = 5120
RANK = 256
GOSSIP_BITS = 4
POS = 192
SECTIONS = 8
REPLICAS = 32


def block_levels(own_key, dims, cuts, low, largest):
    level = 1.0
    for dim, blocks in cuts:
        draws = jax.random.uniform(jax.random.fold_in(jax.random.fold_in(own_key, 6), dim), (blocks,), jnp.float32, low / len(cuts), largest / len(cuts))
        level = level * jnp.repeat(jnp.exp(draws), dims[dim] // blocks).reshape((-1,) + (1,) * (len(dims) - 1 - dim))
    return level


def profile(count, total, reach, lean):
    loads = [(1 << 20) // math.isqrt(standing ** lean) + 1 for standing in range(2, count + 1)]
    rest, counts = total - reach - (count - 1), [1] * (count - 1)
    while rest > 0:
        movable = [i for i in range(count - 1) if counts[i] < reach]
        mass, remaining = sum([loads[i] for i in movable]), rest
        for i in movable:
            addition = min(reach - counts[i], max(1, remaining * loads[i] // mass), rest)
            counts[i] = counts[i] + addition
            rest = rest - addition
    return np.array([reach] + counts)


def ragged(stream_key, amount, total, reach, lean):
    if amount == 2:
        one = jax.random.randint(stream_key, (), max(1, total - reach), min(reach, total - 1) + 1)
        return jnp.stack([one, total - one])
    sizes = jnp.asarray(profile(amount, total, reach, lean), jnp.int32)
    pairs = (amount - 1) // 2
    source_of, receiver = sizes[1:1 + 2 * pairs:2], sizes[2:2 + 2 * pairs:2]
    slack = jnp.minimum(source_of - 1, reach - receiver)
    moved = jax.random.randint(jax.random.fold_in(stream_key, 1), (pairs,), 0, 1 << 20) % (slack + 1)
    sizes = sizes.at[1:1 + 2 * pairs:2].set(source_of - moved).at[2:2 + 2 * pairs:2].set(receiver + moved)
    return sizes[jax.random.permutation(jax.random.fold_in(stream_key, 2), amount)]


def bell_draw(rng, shape, scale, bound, split=(), dtype=jnp.bfloat16):
    level = block_levels(rng, shape, split, -0.22, 0.18) if split else 1.0
    drawn = jax.random.normal(rng, shape, jnp.float32) * scale * level
    return jnp.minimum(jnp.maximum(drawn, -bound), bound).astype(dtype)


def setup_inputs(seed: int = 0) -> dict:
    keys = jax.random.split(jax.random.key(seed), 7)
    stream = bell_draw(keys[0], (REPLICAS, POS, D), 1.0, 6.0, ((0, 32),))
    doc_ids = jax.vmap(lambda own: jnp.searchsorted(jnp.cumsum(ragged(own, POS // 8, POS, POS // 2, 2)), jnp.arange(POS), side="right"))(jax.random.split(keys[1], REPLICAS)).reshape((REPLICAS, POS)).astype(jnp.int32)
    gain = jnp.clip(1.0 + 0.18 * jax.random.normal(keys[2], (REPLICAS, SECTIONS, D), jnp.float32), 0.099609375, 1.8984375).astype(jnp.bfloat16)
    down = bell_draw(keys[3], (REPLICAS, SECTIONS, D, RANK), D ** -0.5, 0.078125, ((0, 32), (1, 8)))
    up = bell_draw(keys[4], (REPLICAS, SECTIONS, D, RANK), RANK ** -0.5, 0.375, ((0, 32), (1, 8)))
    round_exponent = jax.random.randint(keys[5], (1,), 0, 1024).astype(jnp.int32)
    return {"stream": stream, "doc_ids": doc_ids, "gain": gain, "down": down, "up": up, "round_exponent": round_exponent}


EPSILON = 1e-05
LOSS_SCALE = 0.0625

def layer_forward(rows, gain_row, down_w, up_w):
    wide = rows.astype(jnp.float32)
    inverse = lax.rsqrt(lax.optimization_barrier(jnp.mean(wide * wide, axis=-1, keepdims=True)) + EPSILON)
    normed = (wide * inverse * gain_row.astype(jnp.float32)).astype(jnp.bfloat16)
    hidden_pre = jnp.dot(normed, down_w, preferred_element_type=jnp.float32)
    hidden = jax.nn.silu(hidden_pre).astype(jnp.bfloat16)
    update = lax.dot_general(hidden, up_w, (((1,), (1,)), ((), ())), preferred_element_type=jnp.float32)
    return ((wide + update).astype(jnp.bfloat16), normed, hidden_pre, hidden)

def layer_backward(cotangent, rows, hidden_pre, gain_row, down_w, up_w):
    grad_hidden = jnp.dot(cotangent, up_w, preferred_element_type=jnp.float32)
    sigmoid_pre = jax.nn.sigmoid(hidden_pre)
    grad_pre = (grad_hidden * sigmoid_pre * (1.0 + hidden_pre * (1.0 - sigmoid_pre))).astype(jnp.bfloat16)
    grad_normed = lax.dot_general(grad_pre, down_w, (((1,), (1,)), ((), ())), preferred_element_type=jnp.float32)
    wide = rows.astype(jnp.float32)
    inverse = lax.rsqrt(lax.optimization_barrier(jnp.mean(wide * wide, axis=-1, keepdims=True)) + EPSILON)
    scaled = grad_normed * gain_row.astype(jnp.float32)
    inner = lax.optimization_barrier(jnp.mean(scaled * wide, axis=-1, keepdims=True))
    grad_rows = cotangent.astype(jnp.float32) + inverse * (scaled - wide * inverse * inverse * inner)
    return (grad_rows.astype(jnp.bfloat16), grad_pre)

def loss_cotangent(last_rows, target_rows, keep_mask):
    diff = last_rows.astype(jnp.float32) - target_rows.astype(jnp.float32)
    return (LOSS_SCALE * keep_mask[..., None] * diff).astype(jnp.bfloat16)

def reference(stream, doc_ids, gain, down, up, round_exponent):

    def replica_grads(replica):
        rows = lax.dynamic_index_in_dim(stream, replica, 0, keepdims=False)
        docs = lax.dynamic_index_in_dim(doc_ids, replica, 0, keepdims=False)
        gains = lax.dynamic_index_in_dim(gain, replica, 0, keepdims=False)
        downs = lax.dynamic_index_in_dim(down, replica, 0, keepdims=False)
        ups = lax.dynamic_index_in_dim(up, replica, 0, keepdims=False)

        def forward_section(current, weights):
            layer_out, normed, hidden_pre, hidden = layer_forward(current, weights[0], weights[1], weights[2])
            return (layer_out, (current, normed, hidden_pre, hidden))
        last_rows, saved = lax.scan(forward_section, rows, (gains, downs, ups))
        targets = jnp.concatenate([rows[1:], jnp.zeros((1, D), jnp.bfloat16)], axis=0)
        keep_mask = jnp.concatenate([(docs[1:] == docs[:-1]).astype(jnp.float32), jnp.zeros((1,), jnp.float32)])
        first_cot = loss_cotangent(last_rows, targets, keep_mask)

        def backward_section(cotangent, stash):
            inputs_s, normed, hidden_pre, hidden, gain_row, down_w, up_w = stash
            grad_rows, grad_pre = layer_backward(cotangent, inputs_s, hidden_pre, gain_row, down_w, up_w)
            down_grad = jnp.dot(normed.T, grad_pre, preferred_element_type=jnp.float32)
            up_grad = jnp.dot(cotangent.T, hidden, preferred_element_type=jnp.float32)
            return (grad_rows, jnp.stack([down_grad, up_grad]))
        _, section_grads = lax.scan(backward_section, first_cot, saved + (gains, downs, ups), reverse=True)
        return section_grads
    level_bit = jnp.remainder(round_exponent[0], GOSSIP_BITS).astype(jnp.int32)
    distance = jnp.left_shift(jnp.int32(1), level_bit)
    result = jnp.zeros((REPLICAS, SECTIONS, 2, D, RANK), jnp.bfloat16)

    def pair_step(pair_idx, result):
        pair_idx = jnp.asarray(pair_idx).astype(jnp.int32)
        low_part = pair_idx % distance
        lower = (pair_idx - low_part) * 2 + low_part
        upper = lower + distance
        averaged = (0.5 * (replica_grads(lower) + replica_grads(upper))).astype(jnp.bfloat16)
        result = lax.dynamic_update_index_in_dim(result, averaged, lower, 0)
        result = lax.dynamic_update_index_in_dim(result, averaged, upper, 0)
        return result
    return lax.fori_loop(0, REPLICAS // 2, pair_step, result)
```

```python
from functools import partial

import jax
import jax.numpy as jnp
from jax import lax
from jax.experimental import pallas as pl
from jax.experimental.pallas import tpu as pltpu
from jax.sharding import PartitionSpec as P


MICRO = 6
DELAY = 2
CHUNK = 1280
GOSSIP_BITS = 4

EPSILON = 1e-05
LOSS_SCALE = 0.0625


VMEM = pl.BlockSpec(memory_space=pltpu.VMEM)
SMEM = pl.BlockSpec(memory_space=pltpu.SMEM)
ANY = pl.BlockSpec(memory_space=pl.ANY)


def dot(a, b, dims):
    return lax.dot_general(a, b, (dims, ((), ())), preferred_element_type=jnp.float32)


def columns(chunk):
    return pl.ds(pl.multiple_of(chunk * CHUNK, CHUNK), CHUNK)


def keep_rows(docs, keep):
    micro, tok, _ = keep.shape
    last = micro * tok - 1
    row_of = lax.broadcasted_iota(jnp.int32, (tok, 128), 0)
    for slot in range(micro):
        rows = jnp.zeros((tok, 128), jnp.float32)
        for row in range(tok):
            here = slot * tok + row
            if here < last:
                same = docs[0, here + 1] == docs[0, here]
                rows = jnp.where(row_of == row, jnp.where(same, LOSS_SCALE, 0.0), rows)
        keep[slot] = rows


def forward_kernel(tick, sections, has_recv, final, *refs):
    pos, stream, gain, down, up = refs[:5]
    recv = refs[5] if has_recv else None
    docs = None if has_recv else refs[5]
    rows, nh, pre, inv, keep = refs[-5:]
    out = refs[-7] if final else refs[-6]
    micro, tok, width = stream.shape
    rank = down.shape[1]
    pieces = width // CHUNK
    section = pos[0]
    slot = tick - DELAY * section
    is_last = section == sections - 1

    if tick == 0:

        @pl.when(is_last)
        def _():
            keep_rows(docs, keep)

    @pl.when((slot >= 0) & (slot < micro))
    def _():
        @pl.when(section == 0)
        def _():
            rows[slot] = stream[slot]

        if has_recv:

            @pl.when(section != 0)
            def _():
                rows[slot] = recv[...]

        wide = rows[slot].astype(jnp.float32)
        total = jnp.sum(wide * wide, axis=-1, keepdims=True)
        inverse = lax.rsqrt(total / width + EPSILON)
        inv[slot] = jnp.broadcast_to(inverse, (tok, 128))

        def project(piece, total):
            cols = columns(piece)
            wide = rows[slot, :, cols].astype(jnp.float32)
            normed = (wide * inverse * gain[:, cols].astype(jnp.float32)).astype(jnp.bfloat16)
            nh[slot, :, cols] = normed
            return total + dot(normed, down[cols, :], ((1,), (0,)))

        hidden_pre = lax.fori_loop(0, pieces, project, jnp.zeros((tok, rank), jnp.float32))
        pre[slot] = hidden_pre
        hidden = jax.nn.silu(hidden_pre).astype(jnp.bfloat16)
        nh[slot, :, pl.ds(width, rank)] = hidden

        def expand(piece, carry):
            cols = columns(piece)
            update = dot(hidden, up[cols, :], ((1,), (1,)))
            out[:, cols] = (rows[slot, :, cols].astype(jnp.float32) + update).astype(jnp.bfloat16)
            return carry

        lax.fori_loop(0, pieces, expand, 0)

        if tick >= DELAY * (sections - 1):

            @pl.when(is_last)
            def _():
                kept = keep[slot][:, :1]
                after = jnp.minimum(slot + 1, micro - 1)

                def loss(piece, carry):
                    cols = columns(piece)
                    own = stream[slot, :, cols].astype(jnp.float32)
                    edge = stream[after, :, cols].astype(jnp.float32)[:1]
                    rolled = pltpu.roll(own, tok - 1, 0)
                    bottom = lax.broadcasted_iota(jnp.int32, own.shape, 0) == tok - 1
                    target = jnp.where(bottom, edge, rolled)
                    diff = out[:, cols].astype(jnp.float32) - target
                    out[:, cols] = (kept * diff).astype(jnp.bfloat16)
                    return carry

                lax.fori_loop(0, pieces, loss, 0)

    if final:
        refs[-6][...] = nh[...]


def backward_kernel(tick, sections, has_recv, has_own, done, *refs):
    pos, gain, down, up, rows, pre, inv = refs[:7]
    recv = refs[7] if has_recv else None
    own_cot = refs[7 + has_recv] if has_own else None
    cg = refs[-1]
    out = refs[-3] if done >= 0 else refs[-2]
    micro, tok, width = rows.shape
    rank = down.shape[1]
    pieces = width // CHUNK
    section = pos[0]
    slot = tick - DELAY * (sections - 1 - section)

    @pl.when((slot >= 0) & (slot < micro))
    def _():
        if has_recv:

            @pl.when(section != sections - 1)
            def _():
                cg[slot, :, pl.ds(0, width)] = recv[...]

        if has_own:

            @pl.when(section == sections - 1)
            def _():
                cg[slot, :, pl.ds(0, width)] = own_cot[...]

        def contract(piece, total):
            cols = columns(piece)
            return total + dot(cg[slot, :, cols], up[cols, :], ((1,), (0,)))

        grad_hidden = lax.fori_loop(0, pieces, contract, jnp.zeros((tok, rank), jnp.float32))
        hidden_pre = pre[slot]
        sigmoid_pre = jax.nn.sigmoid(hidden_pre)
        grad_pre = grad_hidden * sigmoid_pre * (1.0 + hidden_pre * (1.0 - sigmoid_pre))
        grad_pre = grad_pre.astype(jnp.bfloat16)
        cg[slot, :, pl.ds(width, rank)] = grad_pre

        @pl.when(section != 0)
        def _():
            inverse = inv[slot][:, :1]
            inner = jnp.sum(grad_pre.astype(jnp.float32) * hidden_pre, axis=-1, keepdims=True)
            shrink = inverse * inverse * (inner / width)

            def expand(piece, carry):
                cols = columns(piece)
                grad_normed = dot(grad_pre, down[cols, :], ((1,), (1,)))
                scaled = grad_normed * gain[:, cols].astype(jnp.float32)
                wide = rows[slot, :, cols].astype(jnp.float32)
                own = cg[slot, :, cols].astype(jnp.float32)
                out[:, cols] = (own + (inverse * scaled - wide * shrink)).astype(jnp.bfloat16)
                return carry

            lax.fori_loop(0, pieces, expand, 0)

    if done >= 0:
        refs[-2][...] = cg[done]


def gradient_kernel(micro, *refs):
    n, n_tail, n2, n2_tail = refs[:4]
    parts, parts2 = refs[4 : 4 + micro], refs[4 + micro : 4 + 2 * micro]
    out, c, c2, sems = refs[-4:]
    tok = parts[0].shape[0]
    rank = out.shape[2]
    width = c.shape[1] - rank
    step = pl.program_id(0)
    copies = []
    for kind, (sources, target) in enumerate([(parts, c), (parts2, c2)]):
        for slot, source in enumerate(sources):
            target_rows = target.at[pl.ds(slot * tok, tok)]
            copies.append(pltpu.make_async_copy(source, target_rows, sems.at[kind, slot]))

    @pl.when(step == 0)
    def _():
        for copy in copies:
            copy.start()
        for copy in copies:
            copy.wait()

    first = ((0,), (0,))
    block = out.shape[1]
    cols = pl.ds(pl.multiple_of(step * block, block), block)
    tail = pl.ds(width, rank)
    down_grad = dot(n[...], c[:, tail], first) + dot(n2[...], c2[:, tail], first)
    up_grad = dot(c[:, cols], n_tail[...], first) + dot(c2[:, cols], n2_tail[...], first)
    out[0] = (0.5 * down_grad).astype(jnp.bfloat16)
    out[1] = (0.5 * up_grad).astype(jnp.bfloat16)


def struct(shape, dtype=jnp.bfloat16):
    return pltpu.VMEM(shape, dtype)


def params(mib):
    return pltpu.CompilerParams(vmem_limit_bytes=mib << 20)


def hop(value, step):
    sections = lax.axis_size("section")
    pairs = [(i, i + step) for i in range(sections) if 0 <= i + step < sections]
    return lax.ppermute(value, "section", pairs)


def swap(value, bit):
    count = lax.axis_size("replica")
    return lax.ppermute(value, "replica", [(i, i ^ (1 << bit)) for i in range(count)])


def tick_cost(tok, width, rank):
    return pl.CostEstimate(
        flops=4 * tok * width * rank, bytes_accessed=4 * tok * width, transcendentals=0
    )


def forward(pos, doc_ids, source, gain_row, down_w, up_w):
    sections = lax.axis_size("section")
    _, tok, width = source.shape
    rank = down_w.shape[1]
    ticks = MICRO + DELAY * (sections - 1)
    state_shapes = [
        struct((MICRO, tok, width)),
        struct((MICRO, tok, width + rank)),
        struct((MICRO, tok, rank), jnp.float32),
        struct((MICRO, tok, 128), jnp.float32),
        struct((MICRO, tok, 128), jnp.float32),
    ]
    state, sent, outs = [], [], []
    for tick in range(ticks):
        args = [pos, source, gain_row, down_w, up_w]
        specs = [SMEM] + [VMEM] * 4
        if tick >= DELAY:
            args.append(sent[tick - DELAY])
            specs.append(VMEM)
        else:
            args.append(doc_ids)
            specs.append(SMEM)
        final = tick == ticks - 1
        shapes = [struct((tok, width))] + [state_shapes[1]] * final
        aliases = {len(args) + i: len(shapes) + i for i in range(len(state))}
        out, *state = pl.pallas_call(
            partial(forward_kernel, tick, sections, tick >= DELAY, final),
            out_shape=shapes + state_shapes,
            in_specs=specs + [ANY] * len(state),
            out_specs=[VMEM] * (len(shapes) + len(state_shapes)),
            input_output_aliases=aliases,
            compiler_params=params(8),
            cost_estimate=tick_cost(tok, width, rank),
        )(*args, *state)
        outs.append(out)
        if tick < ticks - DELAY:
            sent.append(hop(out, 1))
    nh, rows, _, pre, inv, _ = state
    return outs[-MICRO:], [rows, nh, pre, inv]


def backward(bit, pos, gain_row, down_w, up_w, last, state):
    sections = lax.axis_size("section")
    rows, nh, pre, inv = state
    _, tok, width = rows.shape
    rank = down_w.shape[1]
    ticks = MICRO + DELAY * (sections - 1)
    cg = []
    sent, parts, parts2 = [], [], []
    out, pending = None, nh.reshape(MICRO * tok, width + rank)
    for tick in range(ticks):
        if 0 < tick <= ticks - DELAY:
            sent.append(hop(out, -1))
        if pending is not None:
            parts2.append(swap(pending, bit))
        args = [pos, gain_row, down_w, up_w, rows, pre, inv]
        if tick >= DELAY:
            args.append(sent[tick - DELAY])
        if tick < MICRO:
            args.append(last[tick])
        done = tick - DELAY * (sections - 1)
        shapes = [struct((tok, width))]
        if done >= 0:
            shapes.append(struct((tok, width + rank)))
        shapes.append(struct((MICRO, tok, width + rank)))
        out, *part, chunk = pl.pallas_call(
            partial(
                backward_kernel, tick, sections, tick >= DELAY, tick < MICRO, done
            ),
            out_shape=shapes,
            in_specs=[SMEM] + [VMEM] * (len(args) - 1) + [ANY] * len(cg),
            out_specs=[VMEM] * len(shapes),
            input_output_aliases={len(args): len(shapes) - 1} if cg else {},
            compiler_params=params(8),
            cost_estimate=tick_cost(tok, width, rank),
        )(*args, *cg)
        cg = [chunk]
        parts += part
        pending = part[0] if part else None
    nh2, *parts2 = parts2 + [swap(pending, bit)]

    positions = MICRO * tok
    block = 512
    major = pl.BlockSpec((positions, block), lambda i: (0, i))
    minor = pl.BlockSpec((positions, rank), lambda i: (0, width // rank))
    stash = pltpu.VMEM((positions, width + rank), jnp.bfloat16)
    nh = nh.reshape(positions, width + rank)
    return pl.pallas_call(
        partial(gradient_kernel, MICRO),
        grid=(width // block,),
        out_shape=jax.ShapeDtypeStruct((2, width, rank), jnp.bfloat16),
        in_specs=[major, minor] * 2 + [ANY] * (2 * MICRO),
        out_specs=pl.BlockSpec((2, block, rank), lambda i: (0, i, 0)),
        scratch_shapes=[stash] * 2 + [pltpu.SemaphoreType.DMA((2, MICRO))],
        compiler_params=params(16),
    )(nh, nh, nh2, nh2, *parts, *parts2)


def shards(stream, doc_ids, gain, down, up, round_exponent):
    pos = lax.axis_index("section").astype(jnp.int32).reshape(1)
    positions, width = stream.shape[1:]
    source = stream[0].reshape(MICRO, positions // MICRO, width)
    weights = [gain[0], down[0, 0], up[0, 0]]
    last, state = forward(pos, doc_ids, source, *weights)
    level_bit = jnp.remainder(round_exponent[0], GOSSIP_BITS)
    branches = [partial(backward, bit) for bit in range(GOSSIP_BITS)]
    return lax.switch(level_bit, branches, pos, *weights, last, state)[None, None]


def solution(mesh):
    placed = (
        P("replica", None, None),
        P("replica", None),
        P("replica", "section", None),
        P("replica", "section", None, None),
        P("replica", "section", None, None),
        P(),
    )
    return jax.shard_map(
        shards,
        mesh=mesh,
        in_specs=placed,
        out_specs=P("replica", "section", None, None, None),
        check_vma=False,
    )
```

```python
from functools import partial

import jax
import jax.numpy as jnp
from jax import lax
from jax.experimental import pallas as pl
from jax.experimental.pallas import tpu as pltpu
from jax.sharding import PartitionSpec as P


MICRO = 8
GROUP = 2
DELAY = 2
CHUNK = 1280
GOSSIP_BITS = 4
PREFIX = (8, 9, 11, 13)

EPSILON = 1e-05
LOSS_SCALE = 0.0625


VMEM = pl.BlockSpec(memory_space=pltpu.VMEM)
SMEM = pl.BlockSpec(memory_space=pltpu.SMEM)
ANY = pl.BlockSpec(memory_space=pl.ANY)


def dot(a, b, dims):
    return lax.dot_general(a, b, (dims, ((), ())), preferred_element_type=jnp.float32)


def columns(chunk):
    return pl.ds(pl.multiple_of(chunk * CHUNK, CHUNK), CHUNK)


def keep_rows(docs, keep):
    micro, tok, _ = keep.shape
    last = micro * tok - 1
    row_of = lax.broadcasted_iota(jnp.int32, (tok, 128), 0)
    for slot in range(micro):
        rows = jnp.zeros((tok, 128), jnp.float32)
        for row in range(tok):
            here = slot * tok + row
            if here < last:
                same = docs[0, here + 1] == docs[0, here]
                rows = jnp.where(row_of == row, jnp.where(same, LOSS_SCALE, 0.0), rows)
        keep[slot] = rows


def forward_kernel(tick, sections, has_recv, *refs):
    pos, stream, gain, down, up = refs[:5]
    recv = refs[5] if has_recv else None
    out, rows, nh, pre, inv, keep = refs[-6:]

    if tick == 0:

        @pl.when(pos[0] == sections - 1)
        def _():
            keep_rows(refs[5], keep)

    forward_step(
        tick, sections, pos, stream, gain, down, up, recv, out, rows, nh, pre, inv, keep
    )


def mixed_kernel(tick, sections, has_back, final, *refs):
    pos, stream, gain, down, up, recv = refs[:6]
    back = refs[6] if has_back else None
    rows, nh, pre, inv, keep, cg = refs[-6:]
    groups = stream.shape[0] // GROUP if final else 0
    out, out_back = refs[-8 - groups], refs[-7 - groups]
    forward_step(
        tick, sections, pos, stream, gain, down, up, recv, out, rows, nh, pre, inv, keep
    )
    start = tick - DELAY * (sections - 1)
    backward_step(
        start, sections, pos, gain, down, up, rows, pre, inv, back, out, out_back, cg
    )
    for group in range(groups):
        refs[group - 6 - groups][...] = nh[pl.ds(group * GROUP, GROUP)]


def forward_step(
    tick, sections, pos, stream, gain, down, up, recv, out, rows, nh, pre, inv, keep
):
    has_recv = recv is not None
    micro, tok, width = stream.shape
    rank = down.shape[1]
    pieces = width // CHUNK
    section = pos[0]
    slot = tick - DELAY * section
    is_last = section == sections - 1

    @pl.when((slot >= 0) & (slot < micro))
    def _():
        def squares(piece, total):
            cols = columns(piece)
            own = stream[slot, :, cols]
            if has_recv:
                own = jnp.where(section == 0, own, recv[:, cols])
            rows[slot, :, cols] = own
            wide = own.astype(jnp.float32)
            return total + jnp.sum(wide * wide, axis=-1, keepdims=True)

        total = lax.fori_loop(0, pieces, squares, jnp.zeros((tok, 1), jnp.float32))
        inverse = lax.rsqrt(total / width + EPSILON)
        inv[slot] = jnp.broadcast_to(inverse, (tok, 128))

        def project(piece, total):
            cols = columns(piece)
            wide = rows[slot, :, cols].astype(jnp.float32)
            normed = (wide * inverse * gain[:, cols].astype(jnp.float32)).astype(jnp.bfloat16)
            nh[slot, :, cols] = normed
            return total + dot(normed, down[cols, :], ((1,), (0,)))

        hidden_pre = lax.fori_loop(0, pieces, project, jnp.zeros((tok, rank), jnp.float32))
        pre[slot] = hidden_pre
        hidden = jax.nn.silu(hidden_pre).astype(jnp.bfloat16)
        nh[slot, :, pl.ds(width, rank)] = hidden

        def expand(piece, carry):
            cols = columns(piece)
            update = dot(hidden, up[cols, :], ((1,), (1,)))
            out[:, cols] = (rows[slot, :, cols].astype(jnp.float32) + update).astype(jnp.bfloat16)
            return carry

        lax.fori_loop(0, pieces, expand, 0)

        if tick >= DELAY * (sections - 1):

            @pl.when(is_last)
            def _():
                kept = keep[slot][:, :1]
                after = jnp.minimum(slot + 1, micro - 1)

                def loss(piece, carry):
                    cols = columns(piece)
                    own = stream[slot, :, cols].astype(jnp.float32)
                    edge = stream[after, :, cols].astype(jnp.float32)[:1]
                    rolled = pltpu.roll(own, tok - 1, 0)
                    bottom = lax.broadcasted_iota(jnp.int32, own.shape, 0) == tok - 1
                    target = jnp.where(bottom, edge, rolled)
                    diff = out[:, cols].astype(jnp.float32) - target
                    out[:, cols] = (kept * diff).astype(jnp.bfloat16)
                    return carry

                lax.fori_loop(0, pieces, loss, 0)


def backward_kernel(tick, sections, done, *refs):
    pos, gain, down, up, rows, pre, inv, recv = refs[:8]
    cg = refs[-1]
    out = refs[-3] if done >= 0 else refs[-2]
    backward_step(tick, sections, pos, gain, down, up, rows, pre, inv, recv, None, out, cg)
    if done >= 0:
        refs[-2][...] = cg[pl.ds(done, GROUP)]


def backward_step(
    tick, sections, pos, gain, down, up, rows, pre, inv, recv, own_cot, out, cg
):
    has_recv, has_own = recv is not None, own_cot is not None
    micro, tok, width = rows.shape
    rank = down.shape[1]
    pieces = width // CHUNK
    section = pos[0]
    slot = tick - DELAY * (sections - 1 - section)

    @pl.when((slot >= 0) & (slot < micro))
    def _():
        def contract(piece, total):
            cols = columns(piece)
            if has_recv and has_own:
                cot = jnp.where(section == sections - 1, own_cot[:, cols], recv[:, cols])
            else:
                cot = recv[:, cols] if has_recv else own_cot[:, cols]
            cg[slot, :, cols] = cot
            return total + dot(cot, up[cols, :], ((1,), (0,)))

        grad_hidden = lax.fori_loop(0, pieces, contract, jnp.zeros((tok, rank), jnp.float32))
        hidden_pre = pre[slot]
        sigmoid_pre = jax.nn.sigmoid(hidden_pre)
        grad_pre = grad_hidden * sigmoid_pre * (1.0 + hidden_pre * (1.0 - sigmoid_pre))
        grad_pre = grad_pre.astype(jnp.bfloat16)
        cg[slot, :, pl.ds(width, rank)] = grad_pre

        @pl.when(section != 0)
        def _():
            inverse = inv[slot][:, :1]
            inner = jnp.sum(grad_pre.astype(jnp.float32) * hidden_pre, axis=-1, keepdims=True)
            shrink = inverse * inverse * (inner / width)

            def expand(piece, carry):
                cols = columns(piece)
                grad_normed = dot(grad_pre, down[cols, :], ((1,), (1,)))
                scaled = grad_normed * gain[:, cols].astype(jnp.float32)
                wide = rows[slot, :, cols].astype(jnp.float32)
                own = cg[slot, :, cols].astype(jnp.float32)
                out[:, cols] = (own + (inverse * scaled - wide * shrink)).astype(jnp.bfloat16)
                return carry

            lax.fori_loop(0, pieces, expand, 0)


def gradient_kernel(groups, *refs):
    sets = [refs[i * groups : (i + 1) * groups] for i in range(4)]
    out, held, sems = refs[4 * groups :]
    rank = out.shape[2]
    width = refs[0].shape[1] - rank
    block = held.shape[2]
    first = ((0,), (0,))

    def stack(parts, span):
        return jnp.concatenate([part[:, span] for part in parts], axis=0)

    h, h2, g, g2 = [stack(parts, pl.ds(width, rank)) for parts in sets]

    def leave(piece, slot):
        rows = pl.ds(pl.multiple_of(piece * block, block), block)
        return pltpu.make_async_copy(held.at[slot], out.at[:, rows], sems.at[slot])

    def step(piece, carry):
        slot = lax.rem(piece, 2)

        @pl.when(piece >= 2)
        def _():
            leave(piece - 2, slot).wait()

        cols = pl.ds(pl.multiple_of(piece * block, block), block)
        n, n2, c, c2 = [stack(parts, cols) for parts in sets]
        down_grad = dot(n, g, first) + dot(n2, g2, first)
        up_grad = dot(c, h, first) + dot(c2, h2, first)
        held[slot, 0] = (0.5 * down_grad).astype(jnp.bfloat16)
        held[slot, 1] = (0.5 * up_grad).astype(jnp.bfloat16)
        leave(piece, slot).start()
        return carry

    pieces = width // block
    lax.fori_loop(0, pieces, step, 0)
    for piece in range(pieces - 2, pieces):
        leave(piece, piece % 2).wait()


def struct(shape, dtype=jnp.bfloat16):
    return pltpu.VMEM(shape, dtype)


def params(mib):
    return pltpu.CompilerParams(vmem_limit_bytes=mib << 20)


def hop(value, step):
    sections = lax.axis_size("section")
    pairs = [(i, i + step) for i in range(sections) if 0 <= i + step < sections]
    return lax.ppermute(value, "section", pairs)


def swap(value, bit):
    count = lax.axis_size("replica")
    return lax.ppermute(value, "replica", [(i, i ^ (1 << bit)) for i in range(count)])


def tick_cost(tok, width, rank):
    return pl.CostEstimate(
        flops=4 * tok * width * rank, bytes_accessed=4 * tok * width, transcendentals=0
    )


def forward(pos, doc_ids, source, gain_row, down_w, up_w):
    sections = lax.axis_size("section")
    _, tok, width = source.shape
    rank = down_w.shape[1]
    ticks = MICRO + DELAY * (sections - 1)
    state_shapes = [
        struct((MICRO, tok, width)),
        struct((MICRO, tok, width + rank)),
        struct((MICRO, tok, rank), jnp.float32),
        struct((MICRO, tok, 128), jnp.float32),
        struct((MICRO, tok, 128), jnp.float32),
    ]
    state, sent = [], []
    turn = DELAY * (sections - 1)
    cost = tick_cost(tok, width, rank)
    for tick in range(turn):
        args = [pos, source, gain_row, down_w, up_w]
        specs = [SMEM] + [VMEM] * 4
        if tick >= DELAY:
            args.append(sent[tick - DELAY])
            specs.append(VMEM)
        else:
            args.append(doc_ids)
            specs.append(SMEM)
        out, *state = pl.pallas_call(
            partial(forward_kernel, tick, sections, tick >= DELAY),
            out_shape=[struct((tok, width))] + state_shapes,
            in_specs=specs + [ANY] * len(state),
            out_specs=[VMEM] * (1 + len(state_shapes)),
            input_output_aliases={len(args) + i: 1 + i for i in range(len(state))},
            compiler_params=params(8),
            cost_estimate=cost,
        )(*args, *state)
        sent.append(hop(out, 1))

    state_shapes = state_shapes + [state_shapes[1]]
    back = []
    for tick in range(turn, ticks):
        final = tick == ticks - 1
        args = [pos, source, gain_row, down_w, up_w, sent[tick - DELAY]]
        if tick >= turn + DELAY:
            args.append(back[tick - turn - DELAY])
        shapes = [struct((tok, width))] * 2
        if final:
            shapes += [struct((GROUP, tok, width + rank))] * (MICRO // GROUP)
        out, out_back, *rest = pl.pallas_call(
            partial(mixed_kernel, tick, sections, tick >= turn + DELAY, final),
            out_shape=shapes + state_shapes,
            in_specs=[SMEM] + [VMEM] * (len(args) - 1) + [ANY] * len(state),
            out_specs=[VMEM] * (len(shapes) + len(state_shapes)),
            input_output_aliases={len(args) + i: len(shapes) + i for i in range(len(state))},
            compiler_params=params(8),
            cost_estimate=cost,
        )(*args, *state)
        state = rest[len(shapes) - 2 :]
        if tick < ticks - DELAY:
            sent.append(hop(out, 1))
        if final:
            back.append(out_back)
        else:
            back.append(hop(out_back, -1))
    rows, _, pre, inv, _, cg = state
    flat = [part.reshape(GROUP * tok, width + rank) for part in rest[: MICRO // GROUP]]
    return back[-DELAY:], [rows, pre, inv], cg, flat


def backward(bit, pos, gain_row, down_w, up_w, back, state, cg, parts):
    sections = lax.axis_size("section")
    rows, pre, inv = state
    _, tok, width = rows.shape
    rank = down_w.shape[1]
    ticks = MICRO + DELAY * (sections - 1)
    span = GROUP * tok
    ends, swapped = [], []
    sent = {MICRO - DELAY: back[0]}
    out = back[1]
    pending = {tick: part for tick, part in zip(PREFIX, parts)}
    for tick in range(MICRO, ticks):
        if tick <= ticks - DELAY:
            sent[tick - 1] = hop(out, -1)
        if tick in pending:
            swapped.append(swap(pending[tick], bit))
        args = [pos, gain_row, down_w, up_w, rows, pre, inv, sent[tick - DELAY]]
        done = tick - DELAY * (sections - 1) - GROUP + 1
        if done % GROUP:
            done = -1
        shapes = [struct((tok, width))]
        if done >= 0:
            shapes.append(struct((GROUP, tok, width + rank)))
        shapes.append(struct((MICRO, tok, width + rank)))
        out, *part, cg = pl.pallas_call(
            partial(backward_kernel, tick, sections, done),
            out_shape=shapes,
            in_specs=[SMEM] + [VMEM] * (len(args) - 1) + [ANY],
            out_specs=[VMEM] * len(shapes),
            input_output_aliases={len(args): len(shapes) - 1},
            compiler_params=params(8),
            cost_estimate=tick_cost(tok, width, rank),
        )(*args, cg)
        if part:
            ends.append(part[0].reshape(span, width + rank))
            pending[tick + 1] = ends[-1]
    swapped.append(swap(ends[-1], bit))

    groups = MICRO // GROUP
    block = 512
    return pl.pallas_call(
        partial(gradient_kernel, groups),
        out_shape=pltpu.HBM((2, width, rank), jnp.bfloat16),
        in_specs=[VMEM] * (4 * groups),
        out_specs=ANY,
        scratch_shapes=[
            pltpu.VMEM((2, 2, block, rank), jnp.bfloat16),
            pltpu.SemaphoreType.DMA((2,)),
        ],
        compiler_params=params(12),
    )(*parts, *swapped[:groups], *ends, *swapped[groups:])


def shards(stream, doc_ids, gain, down, up, round_exponent):
    pos = lax.axis_index("section").astype(jnp.int32).reshape(1)
    positions, width = stream.shape[1:]
    source = stream[0].reshape(MICRO, positions // MICRO, width)
    weights = [gain[0], down[0, 0], up[0, 0]]
    rest = forward(pos, doc_ids, source, *weights)
    level_bit = jnp.remainder(round_exponent[0], GOSSIP_BITS)
    branches = [partial(backward, bit) for bit in range(GOSSIP_BITS)]
    gradients = lax.switch(level_bit, branches, pos, *weights, *rest)
    return gradients[None, None]


def solution(mesh):
    placed = (
        P("replica", None, None),
        P("replica", None),
        P("replica", "section", None),
        P("replica", "section", None, None),
        P("replica", "section", None, None),
        P(),
    )
    return jax.shard_map(
        shards,
        mesh=mesh,
        in_specs=placed,
        out_specs=P("replica", "section", None, None, None),
        check_vma=False,
    )
```

```python
from functools import partial

import jax
import jax.numpy as jnp
from jax import lax
from jax.experimental import pallas as pl
from jax.experimental.pallas import tpu as pltpu
from jax.sharding import PartitionSpec as P


MICRO = 8
GROUP = 2
DELAY = 2
CHUNK = 1280
GOSSIP_BITS = 4
PREFIX = (8, 9, 11, 13)

EPSILON = 1e-05
LOSS_SCALE = 0.0625


VMEM = pl.BlockSpec(memory_space=pltpu.VMEM)
SMEM = pl.BlockSpec(memory_space=pltpu.SMEM)
ANY = pl.BlockSpec(memory_space=pl.ANY)


def dot(a, b, dims):
    return lax.dot_general(a, b, (dims, ((), ())), preferred_element_type=jnp.float32)


def columns(chunk):
    return pl.ds(pl.multiple_of(chunk * CHUNK, CHUNK), CHUNK)


def keep_rows(docs, keep):
    micro, tok, _ = keep.shape
    last = micro * tok - 1
    row_of = lax.broadcasted_iota(jnp.int32, (tok, 128), 0)
    for slot in range(micro):
        rows = jnp.zeros((tok, 128), jnp.float32)
        for row in range(tok):
            here = slot * tok + row
            if here < last:
                same = docs[0, here + 1] == docs[0, here]
                rows = jnp.where(row_of == row, jnp.where(same, LOSS_SCALE, 0.0), rows)
        keep[slot] = rows


def forward_kernel(tick, sections, has_recv, *refs):
    pos, stream, gain, down, up = refs[:5]
    recv = refs[5] if has_recv else None
    out, rows, nh, pre, inv, keep = refs[-6:]

    if tick == 0:

        @pl.when(pos[0] == sections - 1)
        def _():
            keep_rows(refs[5], keep)

    forward_step(
        tick, sections, pos, stream, gain, down, up, recv, out, rows, nh, pre, inv, keep
    )


def mixed_kernel(tick, sections, has_back, final, *refs):
    pos, stream, gain, down, up, recv = refs[:6]
    back = refs[6] if has_back else None
    rows, nh, pre, inv, keep, cg = refs[-6:]
    groups = stream.shape[0] // GROUP if final else 0
    out, out_back = refs[-8 - groups], refs[-7 - groups]
    forward_step(
        tick, sections, pos, stream, gain, down, up, recv, out, rows, nh, pre, inv, keep
    )
    start = tick - DELAY * (sections - 1)
    backward_step(
        start, sections, pos, gain, down, up, rows, pre, inv, back, out, out_back, cg
    )
    for group in range(groups):
        refs[group - 6 - groups][...] = nh[pl.ds(group * GROUP, GROUP)]


def forward_step(
    tick, sections, pos, stream, gain, down, up, recv, out, rows, nh, pre, inv, keep
):
    has_recv = recv is not None
    micro, tok, width = stream.shape
    rank = down.shape[1]
    pieces = width // CHUNK
    section = pos[0]
    slot = tick - DELAY * section
    is_last = section == sections - 1

    @pl.when((slot >= 0) & (slot < micro))
    def _():
        def squares(piece, total):
            cols = columns(piece)
            own = stream[slot, :, cols]
            if has_recv:
                own = jnp.where(section == 0, own, recv[:, cols])
            rows[slot, :, cols] = own
            wide = own.astype(jnp.float32)
            return total + jnp.sum(wide * wide, axis=-1, keepdims=True)

        total = lax.fori_loop(0, pieces, squares, jnp.zeros((tok, 1), jnp.float32))
        inverse = lax.rsqrt(total / width + EPSILON)
        inv[slot] = jnp.broadcast_to(inverse, (tok, 128))

        def project(piece, total):
            cols = columns(piece)
            wide = rows[slot, :, cols].astype(jnp.float32)
            normed = (wide * inverse * gain[:, cols].astype(jnp.float32)).astype(jnp.bfloat16)
            nh[slot, :, cols] = normed
            return total + dot(normed, down[cols, :], ((1,), (0,)))

        hidden_pre = lax.fori_loop(0, pieces, project, jnp.zeros((tok, rank), jnp.float32))
        pre[slot] = hidden_pre
        hidden = jax.nn.silu(hidden_pre).astype(jnp.bfloat16)
        nh[slot, :, pl.ds(width, rank)] = hidden

        def expand(piece, carry):
            cols = columns(piece)
            update = dot(hidden, up[cols, :], ((1,), (1,)))
            out[:, cols] = (rows[slot, :, cols].astype(jnp.float32) + update).astype(jnp.bfloat16)
            return carry

        lax.fori_loop(0, pieces, expand, 0)

        if tick >= DELAY * (sections - 1):

            @pl.when(is_last)
            def _():
                kept = keep[slot][:, :1]
                after = jnp.minimum(slot + 1, micro - 1)

                def loss(piece, carry):
                    cols = columns(piece)
                    own = stream[slot, :, cols].astype(jnp.float32)
                    edge = stream[after, :, cols].astype(jnp.float32)[:1]
                    rolled = pltpu.roll(own, tok - 1, 0)
                    bottom = lax.broadcasted_iota(jnp.int32, own.shape, 0) == tok - 1
                    target = jnp.where(bottom, edge, rolled)
                    diff = out[:, cols].astype(jnp.float32) - target
                    out[:, cols] = (kept * diff).astype(jnp.bfloat16)
                    return carry

                lax.fori_loop(0, pieces, loss, 0)


def backward_kernel(tick, sections, done, *refs):
    pos, gain, down, up, rows, pre, inv, recv = refs[:8]
    cg = refs[-1]
    out = refs[-3] if done >= 0 else refs[-2]
    backward_step(tick, sections, pos, gain, down, up, rows, pre, inv, recv, None, out, cg)
    if done >= 0:
        refs[-2][...] = cg[pl.ds(done, GROUP)]


def backward_step(
    tick, sections, pos, gain, down, up, rows, pre, inv, recv, own_cot, out, cg
):
    has_recv, has_own = recv is not None, own_cot is not None
    micro, tok, width = rows.shape
    rank = down.shape[1]
    pieces = width // CHUNK
    section = pos[0]
    slot = tick - DELAY * (sections - 1 - section)

    @pl.when((slot >= 0) & (slot < micro))
    def _():
        def contract(piece, total):
            cols = columns(piece)
            if has_recv and has_own:
                cot = jnp.where(section == sections - 1, own_cot[:, cols], recv[:, cols])
            else:
                cot = recv[:, cols] if has_recv else own_cot[:, cols]
            cg[slot, :, cols] = cot
            return total + dot(cot, up[cols, :], ((1,), (0,)))

        grad_hidden = lax.fori_loop(0, pieces, contract, jnp.zeros((tok, rank), jnp.float32))
        hidden_pre = pre[slot]
        sigmoid_pre = jax.nn.sigmoid(hidden_pre)
        grad_pre = grad_hidden * sigmoid_pre * (1.0 + hidden_pre * (1.0 - sigmoid_pre))
        grad_pre = grad_pre.astype(jnp.bfloat16)
        cg[slot, :, pl.ds(width, rank)] = grad_pre

        @pl.when(section != 0)
        def _():
            inverse = inv[slot][:, :1]
            inner = jnp.sum(grad_pre.astype(jnp.float32) * hidden_pre, axis=-1, keepdims=True)
            shrink = inverse * inverse * (inner / width)

            def expand(piece, carry):
                cols = columns(piece)
                grad_normed = dot(grad_pre, down[cols, :], ((1,), (1,)))
                scaled = grad_normed * gain[:, cols].astype(jnp.float32)
                wide = rows[slot, :, cols].astype(jnp.float32)
                own = cg[slot, :, cols].astype(jnp.float32)
                out[:, cols] = (own + (inverse * scaled - wide * shrink)).astype(jnp.bfloat16)
                return carry

            lax.fori_loop(0, pieces, expand, 0)


def gradient_kernel(groups, *refs):
    sets = [refs[i * groups : (i + 1) * groups] for i in range(4)]
    out, held, sems = refs[4 * groups :]
    rank = out.shape[2]
    width = refs[0].shape[1] - rank
    block = held.shape[2]
    first = ((0,), (0,))

    def stack(parts, span):
        return jnp.concatenate([part[:, span] for part in parts], axis=0)

    h, h2, g, g2 = [stack(parts, pl.ds(width, rank)) for parts in sets]

    def leave(piece, slot):
        rows = pl.ds(pl.multiple_of(piece * block, block), block)
        return pltpu.make_async_copy(held.at[slot], out.at[:, rows], sems.at[slot])

    def step(piece, carry):
        slot = lax.rem(piece, 2)

        @pl.when(piece >= 2)
        def _():
            leave(piece - 2, slot).wait()

        cols = pl.ds(pl.multiple_of(piece * block, block), block)
        n, n2, c, c2 = [stack(parts, cols) for parts in sets]
        down_grad = dot(n, g, first) + dot(n2, g2, first)
        up_grad = dot(c, h, first) + dot(c2, h2, first)
        held[slot, 0] = (0.5 * down_grad).astype(jnp.bfloat16)
        held[slot, 1] = (0.5 * up_grad).astype(jnp.bfloat16)
        leave(piece, slot).start()
        return carry

    pieces = width // block
    lax.fori_loop(0, pieces, step, 0)
    for piece in range(pieces - 2, pieces):
        leave(piece, piece % 2).wait()


def struct(shape, dtype=jnp.bfloat16):
    return pltpu.VMEM(shape, dtype)


def params(mib):
    return pltpu.CompilerParams(vmem_limit_bytes=mib << 20)


def hop(value, step):
    sections = lax.axis_size("section")
    pairs = [(i, i + step) for i in range(sections) if 0 <= i + step < sections]
    return lax.ppermute(value, "section", pairs)


def swap(value, bit):
    count = lax.axis_size("replica")
    return lax.ppermute(value, "replica", [(i, i ^ (1 << bit)) for i in range(count)])


def tick_cost(tok, width, rank):
    return pl.CostEstimate(
        flops=4 * tok * width * rank, bytes_accessed=4 * tok * width, transcendentals=0
    )


def forward(pos, doc_ids, source, gain_row, down_w, up_w):
    sections = lax.axis_size("section")
    _, tok, width = source.shape
    rank = down_w.shape[1]
    ticks = MICRO + DELAY * (sections - 1)
    state_shapes = [
        struct((MICRO, tok, width)),
        struct((MICRO, tok, width + rank)),
        struct((MICRO, tok, rank), jnp.float32),
        struct((MICRO, tok, 128), jnp.float32),
        struct((MICRO, tok, 128), jnp.float32),
    ]
    state, sent = [], []
    turn = DELAY * (sections - 1)
    cost = tick_cost(tok, width, rank)
    for tick in range(turn):
        args = [pos, source, gain_row, down_w, up_w]
        specs = [SMEM] + [VMEM] * 4
        if tick >= DELAY:
            args.append(sent[tick - DELAY])
            specs.append(VMEM)
        else:
            args.append(doc_ids)
            specs.append(SMEM)
        out, *state = pl.pallas_call(
            partial(forward_kernel, tick, sections, tick >= DELAY),
            out_shape=[struct((tok, width))] + state_shapes,
            in_specs=specs + [ANY] * len(state),
            out_specs=[VMEM] * (1 + len(state_shapes)),
            input_output_aliases={len(args) + i: 1 + i for i in range(len(state))},
            compiler_params=params(8),
            cost_estimate=cost,
        )(*args, *state)
        sent.append(hop(out, 1))

    state_shapes = state_shapes + [state_shapes[1]]
    back = []
    for tick in range(turn, ticks):
        final = tick == ticks - 1
        args = [pos, source, gain_row, down_w, up_w, sent[tick - DELAY]]
        if tick >= turn + DELAY:
            args.append(back[tick - turn - DELAY])
        shapes = [struct((tok, width))] * 2
        if final:
            shapes += [struct((GROUP, tok, width + rank))] * (MICRO // GROUP)
        out, out_back, *rest = pl.pallas_call(
            partial(mixed_kernel, tick, sections, tick >= turn + DELAY, final),
            out_shape=shapes + state_shapes,
            in_specs=[SMEM] + [VMEM] * (len(args) - 1) + [ANY] * len(state),
            out_specs=[VMEM] * (len(shapes) + len(state_shapes)),
            input_output_aliases={len(args) + i: len(shapes) + i for i in range(len(state))},
            compiler_params=params(8),
            cost_estimate=cost,
        )(*args, *state)
        state = rest[len(shapes) - 2 :]
        back.append(out_back if final else hop(out_back, -1))
        if tick < ticks - DELAY:
            sent.append(hop(out, 1))
    rows, _, pre, inv, _, cg = state
    flat = [part.reshape(GROUP * tok, width + rank) for part in rest[: MICRO // GROUP]]
    return back[-DELAY:], [rows, pre, inv], cg, flat


def backward(bit, pos, gain_row, down_w, up_w, back, state, cg, parts):
    sections = lax.axis_size("section")
    rows, pre, inv = state
    _, tok, width = rows.shape
    rank = down_w.shape[1]
    ticks = MICRO + DELAY * (sections - 1)
    span = GROUP * tok
    ends, swapped = [], []
    sent = {MICRO - DELAY: back[0]}
    out = back[1]
    pending = {tick: part for tick, part in zip(PREFIX, parts)}
    for tick in range(MICRO, ticks):
        if tick <= ticks - DELAY:
            sent[tick - 1] = hop(out, -1)
        if tick in pending:
            swapped.append(swap(pending[tick], bit))
        args = [pos, gain_row, down_w, up_w, rows, pre, inv, sent[tick - DELAY]]
        done = tick - DELAY * (sections - 1) - GROUP + 1
        if done % GROUP:
            done = -1
        shapes = [struct((tok, width))]
        if done >= 0:
            shapes.append(struct((GROUP, tok, width + rank)))
        shapes.append(struct((MICRO, tok, width + rank)))
        out, *part, cg = pl.pallas_call(
            partial(backward_kernel, tick, sections, done),
            out_shape=shapes,
            in_specs=[SMEM] + [VMEM] * (len(args) - 1) + [ANY],
            out_specs=[VMEM] * len(shapes),
            input_output_aliases={len(args): len(shapes) - 1},
            compiler_params=params(8),
            cost_estimate=tick_cost(tok, width, rank),
        )(*args, cg)
        if part:
            ends.append(part[0].reshape(span, width + rank))
            pending[tick + 1] = ends[-1]
    swapped.append(swap(ends[-1], bit))

    groups = MICRO // GROUP
    block = 512
    return pl.pallas_call(
        partial(gradient_kernel, groups),
        out_shape=pltpu.HBM((2, width, rank), jnp.bfloat16),
        in_specs=[VMEM] * (4 * groups),
        out_specs=ANY,
        scratch_shapes=[
            pltpu.VMEM((2, 2, block, rank), jnp.bfloat16),
            pltpu.SemaphoreType.DMA((2,)),
        ],
        compiler_params=params(12),
    )(*parts, *swapped[:groups], *ends, *swapped[groups:])


def shards(stream, doc_ids, gain, down, up, round_exponent):
    level_bit = jnp.remainder(round_exponent[0], GOSSIP_BITS)
    early = lax.optimization_barrier(lax.clamp(jnp.int32(0), level_bit, jnp.int32(GOSSIP_BITS - 1)))
    pos = lax.axis_index("section").astype(jnp.int32) + (early >> GOSSIP_BITS)
    pos = pos.reshape(1)
    positions, width = stream.shape[1:]
    source = stream[0].reshape(MICRO, positions // MICRO, width)
    weights = [gain[0], down[0, 0], up[0, 0]]
    rest = forward(pos, doc_ids, source, *weights)
    branches = [partial(backward, bit) for bit in range(GOSSIP_BITS)]
    gradients = lax.switch(level_bit, branches, pos, *weights, *rest)
    return gradients[None, None]


def solution(mesh):
    placed = (
        P("replica", None, None),
        P("replica", None),
        P("replica", "section", None),
        P("replica", "section", None, None),
        P("replica", "section", None, None),
        P(),
    )
    return jax.shard_map(
        shards,
        mesh=mesh,
        in_specs=placed,
        out_specs=P("replica", "section", None, None, None),
        check_vma=False,
    )
```

```python
from functools import partial

import jax
import jax.numpy as jnp
from jax import lax
from jax.experimental import pallas as pl
from jax.experimental.pallas import tpu as pltpu
from jax.sharding import PartitionSpec as P


MICRO = 8
GROUP = 2
DELAY = 2
CHUNK = 1280
GOSSIP_BITS = 4
PREFIX = (8, 9, 11, 13)

EPSILON = 1e-05
LOSS_SCALE = 0.0625


VMEM = pl.BlockSpec(memory_space=pltpu.VMEM)
SMEM = pl.BlockSpec(memory_space=pltpu.SMEM)
ANY = pl.BlockSpec(memory_space=pl.ANY)


def dot(a, b, dims):
    return lax.dot_general(a, b, (dims, ((), ())), preferred_element_type=jnp.float32)


def columns(chunk):
    return pl.ds(pl.multiple_of(chunk * CHUNK, CHUNK), CHUNK)


def keep_rows(docs, keep):
    micro, tok, _ = keep.shape
    last = micro * tok - 1
    row_of = lax.broadcasted_iota(jnp.int32, (tok, 128), 0)
    for slot in range(micro):
        rows = jnp.zeros((tok, 128), jnp.float32)
        for row in range(tok):
            here = slot * tok + row
            if here < last:
                same = docs[0, here + 1] == docs[0, here]
                rows = jnp.where(row_of == row, jnp.where(same, LOSS_SCALE, 0.0), rows)
        keep[slot] = rows


def forward_kernel(tick, sections, has_recv, final, *refs):
    pos, stream, gain, down, up = refs[:5]
    recv = refs[5] if has_recv else None
    rows, nh, pre, inv, keep = refs[-5:]
    groups = stream.shape[0] // GROUP if final else 0
    out = refs[-6 - groups]

    if tick == 0:

        @pl.when(pos[0] == sections - 1)
        def _():
            keep_rows(refs[5], keep)

    forward_step(
        tick, sections, pos, stream, gain, down, up, recv, out, rows, nh, pre, inv, keep
    )
    for group in range(groups):
        refs[group - 5 - groups][...] = nh[pl.ds(group * GROUP, GROUP)]


def turn_kernel(tick, sections, has_recv, *refs):
    pos, gain, down, up, own_cot = refs[:5]
    recv = refs[5] if has_recv else None
    out, rows, pre, inv, cg = refs[-5:]
    backward_step(
        tick, sections, pos, gain, down, up, rows, pre, inv, recv, own_cot, out, cg
    )


def forward_step(
    tick, sections, pos, stream, gain, down, up, recv, out, rows, nh, pre, inv, keep
):
    has_recv = recv is not None
    micro, tok, width = stream.shape
    rank = down.shape[1]
    pieces = width // CHUNK
    section = pos[0]
    slot = tick - DELAY * section
    is_last = section == sections - 1

    @pl.when((slot >= 0) & (slot < micro))
    def _():
        def squares(piece, total):
            cols = columns(piece)
            own = stream[slot, :, cols]
            if has_recv:
                own = jnp.where(section == 0, own, recv[:, cols])
            rows[slot, :, cols] = own
            wide = own.astype(jnp.float32)
            return total + jnp.sum(wide * wide, axis=-1, keepdims=True)

        total = lax.fori_loop(0, pieces, squares, jnp.zeros((tok, 1), jnp.float32))
        inverse = lax.rsqrt(total / width + EPSILON)
        inv[slot] = jnp.broadcast_to(inverse, (tok, 128))

        def project(piece, total):
            cols = columns(piece)
            wide = rows[slot, :, cols].astype(jnp.float32)
            normed = (wide * inverse * gain[:, cols].astype(jnp.float32)).astype(jnp.bfloat16)
            nh[slot, :, cols] = normed
            return total + dot(normed, down[cols, :], ((1,), (0,)))

        hidden_pre = lax.fori_loop(0, pieces, project, jnp.zeros((tok, rank), jnp.float32))
        pre[slot] = hidden_pre
        hidden = jax.nn.silu(hidden_pre).astype(jnp.bfloat16)
        nh[slot, :, pl.ds(width, rank)] = hidden

        def expand(piece, carry):
            cols = columns(piece)
            update = dot(hidden, up[cols, :], ((1,), (1,)))
            out[:, cols] = (rows[slot, :, cols].astype(jnp.float32) + update).astype(jnp.bfloat16)
            return carry

        lax.fori_loop(0, pieces, expand, 0)

        if tick >= DELAY * (sections - 1):

            @pl.when(is_last)
            def _():
                kept = keep[slot][:, :1]
                after = jnp.minimum(slot + 1, micro - 1)

                def loss(piece, carry):
                    cols = columns(piece)
                    own = stream[slot, :, cols].astype(jnp.float32)
                    edge = stream[after, :, cols].astype(jnp.float32)[:1]
                    rolled = pltpu.roll(own, tok - 1, 0)
                    bottom = lax.broadcasted_iota(jnp.int32, own.shape, 0) == tok - 1
                    target = jnp.where(bottom, edge, rolled)
                    diff = out[:, cols].astype(jnp.float32) - target
                    out[:, cols] = (kept * diff).astype(jnp.bfloat16)
                    return carry

                lax.fori_loop(0, pieces, loss, 0)


def backward_kernel(tick, sections, done, *refs):
    pos, gain, down, up, rows, pre, inv, recv = refs[:8]
    cg = refs[-1]
    out = refs[-3] if done >= 0 else refs[-2]
    backward_step(tick, sections, pos, gain, down, up, rows, pre, inv, recv, None, out, cg)
    if done >= 0:
        refs[-2][...] = cg[pl.ds(done, GROUP)]


def backward_step(
    tick, sections, pos, gain, down, up, rows, pre, inv, recv, own_cot, out, cg
):
    has_recv, has_own = recv is not None, own_cot is not None
    micro, tok, width = rows.shape
    rank = down.shape[1]
    pieces = width // CHUNK
    section = pos[0]
    slot = tick - DELAY * (sections - 1 - section)

    @pl.when((slot >= 0) & (slot < micro))
    def _():
        def contract(piece, total):
            cols = columns(piece)
            if has_recv and has_own:
                cot = jnp.where(section == sections - 1, own_cot[:, cols], recv[:, cols])
            else:
                cot = recv[:, cols] if has_recv else own_cot[:, cols]
            cg[slot, :, cols] = cot
            return total + dot(cot, up[cols, :], ((1,), (0,)))

        grad_hidden = lax.fori_loop(0, pieces, contract, jnp.zeros((tok, rank), jnp.float32))
        hidden_pre = pre[slot]
        sigmoid_pre = jax.nn.sigmoid(hidden_pre)
        grad_pre = grad_hidden * sigmoid_pre * (1.0 + hidden_pre * (1.0 - sigmoid_pre))
        grad_pre = grad_pre.astype(jnp.bfloat16)
        cg[slot, :, pl.ds(width, rank)] = grad_pre

        @pl.when(section != 0)
        def _():
            inverse = inv[slot][:, :1]
            inner = jnp.sum(grad_pre.astype(jnp.float32) * hidden_pre, axis=-1, keepdims=True)
            shrink = inverse * inverse * (inner / width)

            def expand(piece, carry):
                cols = columns(piece)
                grad_normed = dot(grad_pre, down[cols, :], ((1,), (1,)))
                scaled = grad_normed * gain[:, cols].astype(jnp.float32)
                wide = rows[slot, :, cols].astype(jnp.float32)
                own = cg[slot, :, cols].astype(jnp.float32)
                out[:, cols] = (own + (inverse * scaled - wide * shrink)).astype(jnp.bfloat16)
                return carry

            lax.fori_loop(0, pieces, expand, 0)


def gradient_kernel(groups, *refs):
    sets = [refs[i * groups : (i + 1) * groups] for i in range(4)]
    out, held, sems = refs[4 * groups :]
    rank = out.shape[2]
    width = refs[0].shape[1] - rank
    block = held.shape[2]
    first = ((0,), (0,))

    def stack(parts, span):
        return jnp.concatenate([part[:, span] for part in parts], axis=0)

    h, h2, g, g2 = [stack(parts, pl.ds(width, rank)) for parts in sets]

    def leave(piece, slot):
        rows = pl.ds(pl.multiple_of(piece * block, block), block)
        return pltpu.make_async_copy(held.at[slot], out.at[:, rows], sems.at[slot])

    def step(piece, carry):
        slot = lax.rem(piece, 2)

        @pl.when(piece >= 2)
        def _():
            leave(piece - 2, slot).wait()

        cols = pl.ds(pl.multiple_of(piece * block, block), block)
        n, n2, c, c2 = [stack(parts, cols) for parts in sets]
        down_grad = dot(n, g, first) + dot(n2, g2, first)
        up_grad = dot(c, h, first) + dot(c2, h2, first)
        held[slot, 0] = (0.5 * down_grad).astype(jnp.bfloat16)
        held[slot, 1] = (0.5 * up_grad).astype(jnp.bfloat16)
        leave(piece, slot).start()
        return carry

    pieces = width // block
    lax.fori_loop(0, pieces, step, 0)
    for piece in range(pieces - 2, pieces):
        leave(piece, piece % 2).wait()


def struct(shape, dtype=jnp.bfloat16):
    return pltpu.VMEM(shape, dtype)


def params(mib):
    return pltpu.CompilerParams(vmem_limit_bytes=mib << 20)


def hop(value, step):
    sections = lax.axis_size("section")
    pairs = [(i, i + step) for i in range(sections) if 0 <= i + step < sections]
    return lax.ppermute(value, "section", pairs)


def swap(value, bit):
    count = lax.axis_size("replica")
    return lax.ppermute(value, "replica", [(i, i ^ (1 << bit)) for i in range(count)])


def tick_cost(tok, width, rank):
    return pl.CostEstimate(
        flops=4 * tok * width * rank, bytes_accessed=4 * tok * width, transcendentals=0
    )


def forward(pos, doc_ids, source, gain_row, down_w, up_w):
    sections = lax.axis_size("section")
    _, tok, width = source.shape
    rank = down_w.shape[1]
    ticks = MICRO + DELAY * (sections - 1)
    state_shapes = [
        struct((MICRO, tok, width)),
        struct((MICRO, tok, width + rank)),
        struct((MICRO, tok, rank), jnp.float32),
        struct((MICRO, tok, 128), jnp.float32),
        struct((MICRO, tok, 128), jnp.float32),
    ]
    state, sent, back, cg = [], [], [], []
    turn = DELAY * (sections - 1)
    cost = tick_cost(tok, width, rank)
    for tick in range(ticks):
        final = tick == ticks - 1
        args = [pos, source, gain_row, down_w, up_w]
        specs = [SMEM] + [VMEM] * 4
        if tick >= DELAY:
            args.append(sent[tick - DELAY])
            specs.append(VMEM)
        else:
            args.append(doc_ids)
            specs.append(SMEM)
        shapes = [struct((tok, width))]
        if final:
            shapes += [struct((GROUP, tok, width + rank))] * (MICRO // GROUP)
        out, *rest = pl.pallas_call(
            partial(forward_kernel, tick, sections, tick >= DELAY, final),
            out_shape=shapes + state_shapes,
            in_specs=specs + [ANY] * len(state),
            out_specs=[VMEM] * (len(shapes) + len(state_shapes)),
            input_output_aliases={len(args) + i: len(shapes) + i for i in range(len(state))},
            compiler_params=params(8),
            cost_estimate=cost,
        )(*args, *state)
        state = rest[len(shapes) - 1 :]
        if tick < ticks - DELAY:
            sent.append(hop(out, 1))
        if tick < turn:
            continue
        rows, nh, pre, inv, keep = state
        args = [pos, gain_row, down_w, up_w, out]
        if tick >= turn + DELAY:
            args.append(back[tick - turn - DELAY])
        held = [rows, pre, inv] + cg
        out_back, rows, pre, inv, chunk = pl.pallas_call(
            partial(turn_kernel, tick - turn, sections, tick >= turn + DELAY),
            out_shape=[struct((tok, width))] + [state_shapes[i] for i in (0, 2, 3, 1)],
            in_specs=[SMEM] + [VMEM] * (len(args) - 1) + [ANY] * len(held),
            out_specs=[VMEM] * 5,
            input_output_aliases={len(args) + i: 1 + i for i in range(len(held))},
            compiler_params=params(8),
            cost_estimate=cost,
        )(*args, *held)
        state, cg = [rows, nh, pre, inv, keep], [chunk]
        back.append(out_back if final else hop(out_back, -1))
    rows, _, pre, inv, _ = state
    flat = [part.reshape(GROUP * tok, width + rank) for part in rest[: MICRO // GROUP]]
    return back[-DELAY:], [rows, pre, inv], cg[0], flat


def backward(bit, pos, gain_row, down_w, up_w, back, state, cg, parts):
    sections = lax.axis_size("section")
    rows, pre, inv = state
    _, tok, width = rows.shape
    rank = down_w.shape[1]
    ticks = MICRO + DELAY * (sections - 1)
    span = GROUP * tok
    ends, swapped = [], []
    sent = {MICRO - DELAY: back[0]}
    out = back[1]
    pending = {tick: part for tick, part in zip(PREFIX, parts)}
    for tick in range(MICRO, ticks):
        if tick <= ticks - DELAY:
            sent[tick - 1] = hop(out, -1)
        if tick in pending:
            swapped.append(swap(pending[tick], bit))
        args = [pos, gain_row, down_w, up_w, rows, pre, inv, sent[tick - DELAY]]
        done = tick - DELAY * (sections - 1) - GROUP + 1
        if done % GROUP:
            done = -1
        shapes = [struct((tok, width))]
        if done >= 0:
            shapes.append(struct((GROUP, tok, width + rank)))
        shapes.append(struct((MICRO, tok, width + rank)))
        out, *part, cg = pl.pallas_call(
            partial(backward_kernel, tick, sections, done),
            out_shape=shapes,
            in_specs=[SMEM] + [VMEM] * (len(args) - 1) + [ANY],
            out_specs=[VMEM] * len(shapes),
            input_output_aliases={len(args): len(shapes) - 1},
            compiler_params=params(8),
            cost_estimate=tick_cost(tok, width, rank),
        )(*args, cg)
        if part:
            ends.append(part[0].reshape(span, width + rank))
            pending[tick + 1] = ends[-1]
    swapped.append(swap(ends[-1], bit))

    groups = MICRO // GROUP
    block = 512
    return pl.pallas_call(
        partial(gradient_kernel, groups),
        out_shape=pltpu.HBM((2, width, rank), jnp.bfloat16),
        in_specs=[VMEM] * (4 * groups),
        out_specs=ANY,
        scratch_shapes=[
            pltpu.VMEM((2, 2, block, rank), jnp.bfloat16),
            pltpu.SemaphoreType.DMA((2,)),
        ],
        compiler_params=params(12),
    )(*parts, *swapped[:groups], *ends, *swapped[groups:])


def shards(stream, doc_ids, gain, down, up, round_exponent):
    level_bit = jnp.remainder(round_exponent[0], GOSSIP_BITS)
    early = lax.optimization_barrier(lax.clamp(jnp.int32(0), level_bit, jnp.int32(GOSSIP_BITS - 1)))
    pos = lax.axis_index("section").astype(jnp.int32) + (early >> GOSSIP_BITS)
    pos = pos.reshape(1)
    positions, width = stream.shape[1:]
    source = stream[0].reshape(MICRO, positions // MICRO, width)
    weights = [gain[0], down[0, 0], up[0, 0]]
    rest = forward(pos, doc_ids, source, *weights)
    branches = [partial(backward, bit) for bit in range(GOSSIP_BITS)]
    gradients = lax.switch(level_bit, branches, pos, *weights, *rest)
    return gradients[None, None]


def solution(mesh):
    placed = (
        P("replica", None, None),
        P("replica", None),
        P("replica", "section", None),
        P("replica", "section", None, None),
        P("replica", "section", None, None),
        P(),
    )
    return jax.shard_map(
        shards,
        mesh=mesh,
        in_specs=placed,
        out_specs=P("replica", "section", None, None, None),
        check_vma=False,
    )
```

```python
from functools import partial

import jax
import jax.numpy as jnp
from jax import lax
from jax.experimental import pallas as pl
from jax.experimental.pallas import tpu as pltpu
from jax.sharding import PartitionSpec as P


MICRO = 8
GROUP = 2
DELAY = 2
CHUNK = 1280
GOSSIP_BITS = 4
PREFIX = (8, 9, 11, 13)

EPSILON = 1e-05
LOSS_SCALE = 0.0625


VMEM = pl.BlockSpec(memory_space=pltpu.VMEM)
SMEM = pl.BlockSpec(memory_space=pltpu.SMEM)
ANY = pl.BlockSpec(memory_space=pl.ANY)


def dot(a, b, dims):
    return lax.dot_general(a, b, (dims, ((), ())), preferred_element_type=jnp.float32)


def columns(chunk):
    return pl.ds(pl.multiple_of(chunk * CHUNK, CHUNK), CHUNK)


def keep_rows(docs, keep):
    micro, tok, _ = keep.shape
    last = micro * tok - 1
    row_of = lax.broadcasted_iota(jnp.int32, (tok, 128), 0)
    for slot in range(micro):
        rows = jnp.zeros((tok, 128), jnp.float32)
        for row in range(tok):
            here = slot * tok + row
            if here < last:
                same = docs[0, here + 1] == docs[0, here]
                rows = jnp.where(row_of == row, jnp.where(same, LOSS_SCALE, 0.0), rows)
        keep[slot] = rows


def forward_kernel(tick, sections, has_recv, final, *refs):
    pos, stream, gain, down, up = refs[:5]
    recv = refs[5] if has_recv else None
    rows, nh, pre, inv, keep = refs[-5:]
    groups = stream.shape[0] // GROUP if final else 0
    out = refs[-6 - groups]

    if tick == 0:

        @pl.when(pos[0] == sections - 1)
        def _():
            keep_rows(refs[5], keep)

    forward_step(
        tick, sections, pos, stream, gain, down, up, recv, out, rows, nh, pre, inv, keep
    )
    for group in range(groups):
        refs[group - 5 - groups][...] = nh[pl.ds(group * GROUP, GROUP)]


def turn_kernel(tick, sections, has_recv, *refs):
    pos, gain, down, up, own_cot = refs[:5]
    recv = refs[5] if has_recv else None
    out, rows, pre, inv, cg = refs[-5:]
    backward_step(
        tick, sections, pos, gain, down, up, rows, pre, inv, recv, own_cot, out, cg
    )


def forward_step(
    tick, sections, pos, stream, gain, down, up, recv, out, rows, nh, pre, inv, keep
):
    has_recv = recv is not None
    micro, tok, width = stream.shape
    rank = down.shape[1]
    pieces = width // CHUNK
    section = pos[0]
    slot = tick - DELAY * section
    is_last = section == sections - 1

    @pl.when((slot >= 0) & (slot < micro))
    def _():
        def project(piece, totals):
            total, product = totals
            cols = columns(piece)
            own = stream[slot, :, cols]
            if has_recv:
                own = jnp.where(section == 0, own, recv[:, cols])
            rows[slot, :, cols] = own
            wide = own.astype(jnp.float32)
            scaled = (wide * gain[:, cols].astype(jnp.float32)).astype(jnp.bfloat16)
            total = total + jnp.sum(wide * wide, axis=-1, keepdims=True)
            return total, product + dot(scaled, down[cols, :], ((1,), (0,)))

        zeros = jnp.zeros((tok, 1), jnp.float32), jnp.zeros((tok, rank), jnp.float32)
        total, product = lax.fori_loop(0, pieces, project, zeros)
        inverse = lax.rsqrt(total / width + EPSILON)
        inv[slot] = jnp.broadcast_to(inverse, (tok, 128))
        hidden_pre = product * inverse
        pre[slot] = hidden_pre
        hidden = jax.nn.silu(hidden_pre).astype(jnp.bfloat16)
        nh[slot, :, pl.ds(width, rank)] = hidden

        def expand(piece, carry):
            cols = columns(piece)
            update = dot(hidden, up[cols, :], ((1,), (1,)))
            wide = rows[slot, :, cols].astype(jnp.float32)
            normed = wide * inverse * gain[:, cols].astype(jnp.float32)
            nh[slot, :, cols] = normed.astype(jnp.bfloat16)
            out[:, cols] = (wide + update).astype(jnp.bfloat16)
            return carry

        lax.fori_loop(0, pieces, expand, 0)

        if tick >= DELAY * (sections - 1):

            @pl.when(is_last)
            def _():
                kept = keep[slot][:, :1]
                after = jnp.minimum(slot + 1, micro - 1)

                def loss(piece, carry):
                    cols = columns(piece)
                    own = stream[slot, :, cols].astype(jnp.float32)
                    edge = stream[after, :, cols].astype(jnp.float32)[:1]
                    rolled = pltpu.roll(own, tok - 1, 0)
                    bottom = lax.broadcasted_iota(jnp.int32, own.shape, 0) == tok - 1
                    target = jnp.where(bottom, edge, rolled)
                    diff = out[:, cols].astype(jnp.float32) - target
                    out[:, cols] = (kept * diff).astype(jnp.bfloat16)
                    return carry

                lax.fori_loop(0, pieces, loss, 0)


def backward_kernel(tick, sections, done, *refs):
    pos, gain, down, up, rows, pre, inv, recv = refs[:8]
    cg = refs[-1]
    out = refs[-3] if done >= 0 else refs[-2]
    backward_step(tick, sections, pos, gain, down, up, rows, pre, inv, recv, None, out, cg)
    if done >= 0:
        refs[-2][...] = cg[pl.ds(done, GROUP)]


def backward_step(
    tick, sections, pos, gain, down, up, rows, pre, inv, recv, own_cot, out, cg
):
    has_recv, has_own = recv is not None, own_cot is not None
    micro, tok, width = rows.shape
    rank = down.shape[1]
    pieces = width // CHUNK
    section = pos[0]
    slot = tick - DELAY * (sections - 1 - section)

    @pl.when((slot >= 0) & (slot < micro))
    def _():
        def contract(piece, total):
            cols = columns(piece)
            if has_recv and has_own:
                cot = jnp.where(section == sections - 1, own_cot[:, cols], recv[:, cols])
            else:
                cot = recv[:, cols] if has_recv else own_cot[:, cols]
            cg[slot, :, cols] = cot
            return total + dot(cot, up[cols, :], ((1,), (0,)))

        grad_hidden = lax.fori_loop(0, pieces, contract, jnp.zeros((tok, rank), jnp.float32))
        hidden_pre = pre[slot]
        sigmoid_pre = jax.nn.sigmoid(hidden_pre)
        grad_pre = grad_hidden * sigmoid_pre * (1.0 + hidden_pre * (1.0 - sigmoid_pre))
        grad_pre = grad_pre.astype(jnp.bfloat16)
        cg[slot, :, pl.ds(width, rank)] = grad_pre

        @pl.when(section != 0)
        def _():
            inverse = inv[slot][:, :1]
            inner = jnp.sum(grad_pre.astype(jnp.float32) * hidden_pre, axis=-1, keepdims=True)
            shrink = inverse * inverse * (inner / width)

            def expand(piece, carry):
                cols = columns(piece)
                grad_normed = dot(grad_pre, down[cols, :], ((1,), (1,)))
                scaled = grad_normed * gain[:, cols].astype(jnp.float32)
                wide = rows[slot, :, cols].astype(jnp.float32)
                own = cg[slot, :, cols].astype(jnp.float32)
                out[:, cols] = (own + (inverse * scaled - wide * shrink)).astype(jnp.bfloat16)
                return carry

            lax.fori_loop(0, pieces, expand, 0)


def gradient_kernel(groups, *refs):
    sets = [refs[i * groups : (i + 1) * groups] for i in range(4)]
    out, held, sems = refs[4 * groups :]
    rank = out.shape[2]
    width = refs[0].shape[1] - rank
    block = held.shape[2]
    first = ((0,), (0,))

    def stack(parts, span):
        return jnp.concatenate([part[:, span] for part in parts], axis=0)

    h, h2, g, g2 = [stack(parts, pl.ds(width, rank)) for parts in sets]

    def leave(piece, slot):
        rows = pl.ds(pl.multiple_of(piece * block, block), block)
        return pltpu.make_async_copy(held.at[slot], out.at[:, rows], sems.at[slot])

    def step(piece, carry):
        slot = lax.rem(piece, 2)

        @pl.when(piece >= 2)
        def _():
            leave(piece - 2, slot).wait()

        cols = pl.ds(pl.multiple_of(piece * block, block), block)
        n, n2, c, c2 = [stack(parts, cols) for parts in sets]
        down_grad = dot(n, g, first) + dot(n2, g2, first)
        up_grad = dot(c, h, first) + dot(c2, h2, first)
        held[slot, 0] = (0.5 * down_grad).astype(jnp.bfloat16)
        held[slot, 1] = (0.5 * up_grad).astype(jnp.bfloat16)
        leave(piece, slot).start()
        return carry

    pieces = width // block
    lax.fori_loop(0, pieces, step, 0)
    for piece in range(pieces - 2, pieces):
        leave(piece, piece % 2).wait()


def struct(shape, dtype=jnp.bfloat16):
    return pltpu.VMEM(shape, dtype)


def params(mib):
    return pltpu.CompilerParams(vmem_limit_bytes=mib << 20)


def hop(value, step):
    sections = lax.axis_size("section")
    pairs = [(i, i + step) for i in range(sections) if 0 <= i + step < sections]
    return lax.ppermute(value, "section", pairs)


def swap(value, bit):
    count = lax.axis_size("replica")
    return lax.ppermute(value, "replica", [(i, i ^ (1 << bit)) for i in range(count)])


def tick_cost(tok, width, rank):
    return pl.CostEstimate(
        flops=4 * tok * width * rank, bytes_accessed=4 * tok * width, transcendentals=0
    )


def forward(pos, doc_ids, source, gain_row, down_w, up_w):
    sections = lax.axis_size("section")
    _, tok, width = source.shape
    rank = down_w.shape[1]
    ticks = MICRO + DELAY * (sections - 1)
    state_shapes = [
        struct((MICRO, tok, width)),
        struct((MICRO, tok, width + rank)),
        struct((MICRO, tok, rank), jnp.float32),
        struct((MICRO, tok, 128), jnp.float32),
        struct((MICRO, tok, 128), jnp.float32),
    ]
    state, sent, back, cg = [], [], [], []
    turn = DELAY * (sections - 1)
    cost = tick_cost(tok, width, rank)
    for tick in range(ticks):
        final = tick == ticks - 1
        args = [pos, source, gain_row, down_w, up_w]
        specs = [SMEM] + [VMEM] * 4
        if tick >= DELAY:
            args.append(sent[tick - DELAY])
            specs.append(VMEM)
        else:
            args.append(doc_ids)
            specs.append(SMEM)
        shapes = [struct((tok, width))]
        if final:
            shapes += [struct((GROUP, tok, width + rank))] * (MICRO // GROUP)
        out, *rest = pl.pallas_call(
            partial(forward_kernel, tick, sections, tick >= DELAY, final),
            out_shape=shapes + state_shapes,
            in_specs=specs + [ANY] * len(state),
            out_specs=[VMEM] * (len(shapes) + len(state_shapes)),
            input_output_aliases={len(args) + i: len(shapes) + i for i in range(len(state))},
            compiler_params=params(8),
            cost_estimate=cost,
        )(*args, *state)
        state = rest[len(shapes) - 1 :]
        if tick < ticks - DELAY:
            sent.append(hop(out, 1))
        if tick < turn:
            continue
        rows, nh, pre, inv, keep = state
        args = [pos, gain_row, down_w, up_w, out]
        if tick >= turn + DELAY:
            args.append(back[tick - turn - DELAY])
        held = [rows, pre, inv] + cg
        out_back, rows, pre, inv, chunk = pl.pallas_call(
            partial(turn_kernel, tick - turn, sections, tick >= turn + DELAY),
            out_shape=[struct((tok, width))] + [state_shapes[i] for i in (0, 2, 3, 1)],
            in_specs=[SMEM] + [VMEM] * (len(args) - 1) + [ANY] * len(held),
            out_specs=[VMEM] * 5,
            input_output_aliases={len(args) + i: 1 + i for i in range(len(held))},
            compiler_params=params(8),
            cost_estimate=cost,
        )(*args, *held)
        state, cg = [rows, nh, pre, inv, keep], [chunk]
        back.append(out_back if final else hop(out_back, -1))
    rows, _, pre, inv, _ = state
    flat = [part.reshape(GROUP * tok, width + rank) for part in rest[: MICRO // GROUP]]
    return back[-DELAY:], [rows, pre, inv], cg[0], flat


def backward(bit, pos, gain_row, down_w, up_w, back, state, cg, parts):
    sections = lax.axis_size("section")
    rows, pre, inv = state
    _, tok, width = rows.shape
    rank = down_w.shape[1]
    ticks = MICRO + DELAY * (sections - 1)
    span = GROUP * tok
    ends, swapped = [], []
    sent = {MICRO - DELAY: back[0]}
    out = back[1]
    pending = {tick: part for tick, part in zip(PREFIX, parts)}
    for tick in range(MICRO, ticks):
        if tick <= ticks - DELAY:
            sent[tick - 1] = hop(out, -1)
        if tick in pending:
            swapped.append(swap(pending[tick], bit))
        args = [pos, gain_row, down_w, up_w, rows, pre, inv, sent[tick - DELAY]]
        done = tick - DELAY * (sections - 1) - GROUP + 1
        if done % GROUP:
            done = -1
        shapes = [struct((tok, width))]
        if done >= 0:
            shapes.append(struct((GROUP, tok, width + rank)))
        shapes.append(struct((MICRO, tok, width + rank)))
        out, *part, cg = pl.pallas_call(
            partial(backward_kernel, tick, sections, done),
            out_shape=shapes,
            in_specs=[SMEM] + [VMEM] * (len(args) - 1) + [ANY],
            out_specs=[VMEM] * len(shapes),
            input_output_aliases={len(args): len(shapes) - 1},
            compiler_params=params(8),
            cost_estimate=tick_cost(tok, width, rank),
        )(*args, cg)
        if part:
            ends.append(part[0].reshape(span, width + rank))
            pending[tick + 1] = ends[-1]
    swapped.append(swap(ends[-1], bit))

    groups = MICRO // GROUP
    block = 512
    return pl.pallas_call(
        partial(gradient_kernel, groups),
        out_shape=pltpu.HBM((2, width, rank), jnp.bfloat16),
        in_specs=[VMEM] * (4 * groups),
        out_specs=ANY,
        scratch_shapes=[
            pltpu.VMEM((2, 2, block, rank), jnp.bfloat16),
            pltpu.SemaphoreType.DMA((2,)),
        ],
        compiler_params=params(12),
    )(*parts, *swapped[:groups], *ends, *swapped[groups:])


def shards(stream, doc_ids, gain, down, up, round_exponent):
    level_bit = jnp.remainder(round_exponent[0], GOSSIP_BITS)
    early = lax.optimization_barrier(lax.clamp(jnp.int32(0), level_bit, jnp.int32(GOSSIP_BITS - 1)))
    pos = lax.axis_index("section").astype(jnp.int32) + (early >> GOSSIP_BITS)
    pos = pos.reshape(1)
    positions, width = stream.shape[1:]
    source = stream[0].reshape(MICRO, positions // MICRO, width)
    weights = [gain[0], down[0, 0], up[0, 0]]
    rest = forward(pos, doc_ids, source, *weights)
    branches = [partial(backward, bit) for bit in range(GOSSIP_BITS)]
    gradients = lax.switch(level_bit, branches, pos, *weights, *rest)
    return gradients[None, None]


def solution(mesh):
    placed = (
        P("replica", None, None),
        P("replica", None),
        P("replica", "section", None),
        P("replica", "section", None, None),
        P("replica", "section", None, None),
        P(),
    )
    return jax.shard_map(
        shards,
        mesh=mesh,
        in_specs=placed,
        out_specs=P("replica", "section", None, None, None),
        check_vma=False,
    )
```
